128 devices in a mesh: row: 16 (over x, z), col: 8 (over y, core).
Axes of the slice: x: 4, y: 4, z: 4, core: 2. Of those that a mesh axis runs over, the one named last changes fastest.
Arguments:
- front: float32 [6, 2048, 12, 1024], P(None, 'row', None, 'col')
- children: float32 [32768, 8192], P('row', 'col')
- block_map: int32 [4, 64], replicated, may hold values from -1 to 95, as said below
- child_at: int32 [4], replicated, may hold values from 0 to 3, each once
Outputs:
- factored: float32 [6, 2048, 12, 1024], P(None, 'row', None, 'col')
The draws below stay inside these ranges and needn't reach their ends.
Inputs may be any that keep to these rules, and one draw needn't show every extreme that they name: Entry block_map[k, t * 16 + p] is -1 or a parent block b with b % 16 == p. For each child k and each p the entries that are not -1 come first in t, increase, and number 4 // 2 to 4; for every child both of these counts occur. No block appears twice for one child. `child_at`: each child stands in exactly one slot.
All inputs are finite; a program needn't handle non-finite values.
Results may differ from the reference program's by a relative error of at most 0.00005.
Values sent between devices are 32-bit elements; how exact they have to be, the bound alone decides.
A program may use at most 192 MiB of HBM per device.

```python
import math
import jax
import jax.numpy as jnp
from jax import lax

BS = 128
NBLK = 96
CHILD = 4
PB = 8
LBR = 6
LBC = 12
CAPR = 4
RSLOTS = 64
CSLOTS = 64
ROW_SPAN = 2048
COL_SPAN = 1024


def draw_front(key, part):
    array_shape = (LBR, ROW_SPAN, LBC, COL_SPAN)
    noise_key = jax.random.fold_in(key, 11)
    boost_key = jax.random.fold_in(key, 12)
    noise_part = jnp.clip(jax.random.normal(noise_key, array_shape, jnp.float32), -6.0, 6.0)
    diag_boost = jax.random.uniform(boost_key, array_shape, jnp.float32, 8.0, 16.0) * math.sqrt(PB * BS)
    row_ids = jnp.arange(LBR)[:, None, None, None] * ROW_SPAN + jnp.arange(ROW_SPAN)[None, :, None, None]
    col_ids = jnp.arange(LBC)[None, None, :, None] * COL_SPAN + jnp.arange(COL_SPAN)[None, None, None, :]
    return noise_part + jnp.where(row_ids == col_ids, diag_boost, 0.0)


def draw_children(key, part):
    array_shape = (CHILD * RSLOTS * BS, CSLOTS * BS)
    value_key = jax.random.fold_in(key, 22)
    return jnp.clip(jax.random.normal(value_key, array_shape, jnp.float32), -6.0, 6.0)


def draw_block_map(key, part):
    groups = RSLOTS // CAPR
    counts = jax.random.randint(jax.random.fold_in(key, 31), (CHILD, groups), CAPR // 2, CAPR + 1)
    low_owner = jax.random.randint(jax.random.fold_in(key, 32), (CHILD,), 0, groups)
    high_owner = (low_owner + 1 + jax.random.randint(jax.random.fold_in(key, 33), (CHILD,), 0, groups - 1)) % groups
    owner_ids = jnp.arange(groups)[None, :]
    counts = jnp.where(owner_ids == low_owner[:, None], CAPR // 2, counts)
    counts = jnp.where(owner_ids == high_owner[:, None], CAPR, counts)
    subkeys = jax.random.split(jax.random.fold_in(key, 34), CHILD * groups)
    permuted = jax.vmap(lambda subkey: jax.random.permutation(subkey, LBR))(subkeys)
    permuted = permuted.reshape(CHILD, groups, LBR)[:, :, :CAPR]
    slot_ids = jnp.arange(CAPR)[None, None, :]
    chosen = jnp.sort(jnp.where(slot_ids < counts[:, :, None], permuted, LBR), axis=2)
    mapped = jnp.where(chosen < LBR, chosen * groups + owner_ids[:, :, None], -1)
    return mapped.transpose(0, 2, 1).reshape(CHILD, CAPR * groups).astype(jnp.int32)


def setup_inputs(seed: int = 0) -> dict:
    key_of = jax.random.split(jax.random.key(seed), 5)
    return {
        "front": draw_front(jax.random.fold_in(key_of[4], 71), 0),
        "children": draw_children(jax.random.fold_in(key_of[4], 71), 0),
        "block_map": draw_block_map(jax.random.fold_in(key_of[4], 71), 0),
        "child_at": jax.random.permutation(key_of[3], CHILD).astype(jnp.int32),
    }


def reference(front, children, block_map, child_at):
    grid_rows = ROW_SPAN // BS
    grid_cols = COL_SPAN // BS
    fanout = grid_rows // grid_cols
    front_order = NBLK * BS
    panel_width = PB * BS
    blocks = front.reshape(NBLK, BS, NBLK, BS)
    pieces = children.reshape(CHILD, RSLOTS, BS, CSLOTS, BS)
    for slot_index in range(CHILD):
        mapping = block_map[child_at[slot_index]]
        columns = mapping.reshape(CAPR, fanout, grid_cols).transpose(2, 1, 0).reshape(CSLOTS)
        rows_to = jnp.where(mapping >= 0, mapping, NBLK).astype(jnp.int32)
        cols_to = jnp.where(columns >= 0, columns, NBLK).astype(jnp.int32)
        blocks = blocks.at[rows_to[:, None], :, cols_to[None, :], :].add(pieces[slot_index].transpose(0, 2, 1, 3), mode='drop')
    whole = blocks.reshape(front_order, front_order)
    corner = whole[:panel_width, :panel_width]
    factor = jnp.tril(jnp.linalg.cholesky(0.5 * (corner + corner.T)))
    lower_part = jax.scipy.linalg.solve_triangular(factor, whole[panel_width:, :panel_width].T, lower=True).T
    trailing = whole[panel_width:, panel_width:] - jnp.dot(lower_part, lower_part.T, precision=lax.Precision.HIGHEST)
    result = whole.at[:panel_width, :panel_width].set(factor)
    result = result.at[panel_width:, :panel_width].set(lower_part)
    result = result.at[panel_width:, panel_width:].set(trailing)
    return result.reshape(LBR, ROW_SPAN, LBC, COL_SPAN)
```

```python
import functools
import jax
import jax.numpy as jnp
from jax import lax
from jax.experimental import pallas as pl
from jax.experimental.pallas import tpu as pltpu
from jax.sharding import PartitionSpec as P

F32 = jnp.float32
BF16 = jnp.bfloat16
HIGHEST = lax.Precision.HIGHEST
CHILD = 4
BS = 128
NT = ((1,), (1,))
NN = ((1,), (0,))
VMEM_SPEC = pl.BlockSpec(memory_space=pltpu.VMEM)
SMEM_SPEC = pl.BlockSpec(memory_space=pltpu.SMEM)


def mm(a, b, dims):
    return lax.dot_general(a, b, (dims, ((), ())), precision=HIGHEST, preferred_element_type=F32)


def split(x):
    hi = x.astype(BF16)
    return hi, (x - hi.astype(F32)).astype(BF16)


def mm3(a, b, dims):
    dot = functools.partial(
        lax.dot_general, dimension_numbers=(dims, ((), ())), preferred_element_type=F32
    )
    return dot(a[0], b[0]) + (dot(a[0], b[1]) + dot(a[1], b[0]))


def diag_factor(get, put_u, put_x):
    sub = lax.broadcasted_iota(jnp.int32, (8, 128), 0)
    lane = lax.broadcasted_iota(jnp.int32, (8, 128), 1)
    d = [get(i) for i in range(16)]
    x = [(lane == sub + 8 * i).astype(F32) for i in range(16)]

    def panel(i, carry):
        d, x = list(carry[0]), list(carry[1])
        for j in range(8):
            c0 = jnp.broadcast_to(d[0][:, j:j + 1], (8, 128))
            r = lax.rsqrt(jnp.broadcast_to(c0[j:j + 1, :], (8, 128)))
            ud = jnp.broadcast_to(d[0][j:j + 1, :], (8, 128)) * r
            ux = jnp.broadcast_to(x[0][j:j + 1, :], (8, 128)) * r
            m = jnp.where(sub > j, c0 * r, 0.0)
            d[0] = jnp.where(sub == j, ud, d[0] - m * ud)
            x[0] = jnp.where(sub == j, ux, x[0] - m * ux)
            for k in range(1, 16):
                m = jnp.broadcast_to(d[k][:, j:j + 1], (8, 128)) * r
                d[k] = d[k] - m * ud
                x[k] = x[k] - m * ux
        row = d[0]
        row = pltpu.roll(row, 8 * i, 1)
        put_u(i, jnp.where(lane >= sub + 8 * i, row, 0.0))
        put_x(i, x[0])
        nd = [pltpu.roll(v, 120, 1) for v in d[1:]] + [jnp.zeros((8, 128), F32)]
        nx = x[1:] + [jnp.zeros((8, 128), F32)]
        return tuple(nd), tuple(nx)

    lax.fori_loop(0, 16, panel, (tuple(d), tuple(x)))


def chol_kernel(n, c_ref, l_ref, m_ref, u_ref, x_ref):
    def blk(i, j):
        return (pl.ds(i * BS, BS), pl.ds(j * BS, BS))

    def corner(i, j):
        return jnp.concatenate([c_ref[i * n + j], c_ref[(i + n) * n + j]], axis=0)

    for i in range(n):
        for j in range(i + 1):
            l_ref[blk(i, j)] = 0.5 * (corner(i, j) + corner(j, i).T)
        for j in range(i + 1, n):
            l_ref[blk(i, j)] = jnp.zeros((BS, BS), F32)

    def put_u(i, v):
        u_ref[pl.ds(pl.multiple_of(8 * i, 8), 8), :] = v

    def put_x(i, v):
        x_ref[pl.ds(pl.multiple_of(8 * i, 8), 8), :] = v

    for k in range(n):
        diag_factor(lambda i, k=k: l_ref[pl.ds(k * BS + 8 * i, 8), pl.ds(k * BS, BS)], put_u, put_x)
        l_ref[blk(k, k)] = u_ref[...].T
        x = x_ref[...]
        h = k % 2
        m_ref[k // 2, h * BS : (h + 1) * BS, h * BS : (h + 1) * BS] = x
        if h == 1:
            m_ref[k // 2, 0:BS, BS : 2 * BS] = jnp.zeros((BS, BS), F32)
            t = mm(l_ref[blk(k, k - 1)], m_ref[k // 2, 0:BS, 0:BS], NN)
            m_ref[k // 2, BS : 2 * BS, 0:BS] = -mm(x, t, NN)
        if k + 1 < n:
            lo = (k + 1) * BS
            rest = n * BS - lo
            col = mm(l_ref[pl.ds(lo, rest), pl.ds(k * BS, BS)], x, NT)
            l_ref[pl.ds(lo, rest), pl.ds(k * BS, BS)] = col
            for j in range(k + 1, n):
                o = (j - k - 1) * BS
                l_ref[pl.ds(j * BS, n * BS - j * BS), pl.ds(j * BS, BS)] -= mm(
                    col[o:], col[o : o + BS], NT
                )


def cholesky(corner):
    n = 8
    return pl.pallas_call(
        functools.partial(chol_kernel, n),
        out_shape=(
            jax.ShapeDtypeStruct((n * BS, n * BS), F32),
            jax.ShapeDtypeStruct((n // 2, 2 * BS, 2 * BS), F32),
        ),
        in_specs=[VMEM_SPEC],
        out_specs=(VMEM_SPEC, VMEM_SPEC),
        scratch_shapes=[pltpu.VMEM((BS, BS), F32), pltpu.VMEM((BS, BS), F32)],
        cost_estimate=pl.CostEstimate(
            flops=100_000_000_000, bytes_accessed=9_000_000, transcendentals=0
        ),
        name="cholesky",
    )(corner)


def assemble_kernel(bm_ref, at_ref, front_ref, recv_ref, out_ref):
    p = lax.axis_index("row")
    q = lax.axis_index("col")
    out_ref[...] = front_ref[:, 0]
    for c in range(CHILD):
        k = at_ref[c]
        hit = bm_ref[k, q] == q
        for t in range(4):
            r = bm_ref[k, t * 16 + p]

            @pl.when(jnp.logical_and(hit, r >= 0))
            def _(r=r, s=c * 4 + t):
                out_ref[r >> 4] += recv_ref[s]


def assemble_panel(block_map, child_at, front, recv):
    return pl.pallas_call(
        assemble_kernel,
        grid=(1,),
        out_shape=jax.ShapeDtypeStruct((6, BS, BS), F32),
        in_specs=[
            SMEM_SPEC,
            SMEM_SPEC,
            pl.BlockSpec((6, 1, BS, BS), lambda i: (0, 0, 0, 0)),
            pl.BlockSpec((16, BS, BS), lambda i: (0, 0, 0)),
        ],
        out_specs=pl.BlockSpec((6, BS, BS), lambda i: (0, 0, 0)),
        name="assemble_panel",
    )(block_map, child_at, front, recv)


def update_kernel(
    bm_ref, at_ref, front_ref, recv0_ref, recv1_ref, rrow_ref, rcol_ref, l_ref, m_ref, out_ref,
    lh_ref, ll_ref, mh_ref, ml_ref, yf_ref, yh_ref, yl_ref, zh_ref, zl_ref,
):
    step = pl.program_id(0)
    p = lax.axis_index("row")
    q = lax.axis_index("col")
    W = 2 * BS

    def solve(rhs, rows, yh, yl, yf):
        for k in range(4):
            t = rhs(k)
            for j in range(k):
                js = pl.ds(j * W, W)
                ks = pl.ds(k * W, W)
                t = t - mm3((yh[:, js], yl[:, js]), (lh_ref[ks, js], ll_ref[ks, js]), NT)
            y = mm3(split(t), (mh_ref[k], ml_ref[k]), NT)
            ks = pl.ds(k * W, W)
            if yf is not None:
                yf[:, ks] = y
            yh[:, ks], yl[:, ks] = split(y)

    @pl.when(step == 0)
    def _():
        for k in range(4):
            mh_ref[k], ml_ref[k] = split(m_ref[k])
            for j in range(k):
                js = pl.ds(j * W, W)
                ks = pl.ds(k * W, W)
                lh_ref[ks, js], ll_ref[ks, js] = split(l_ref[ks, js])
        solve(
            lambda k: jnp.concatenate([rrow_ref[2 * k], rrow_ref[2 * k + 1]], axis=1),
            768, yh_ref, yl_ref, yf_ref,
        )

    def rcol(k):
        return jnp.concatenate(
            [
                jnp.concatenate([rcol_ref[8 * e + 2 * k], rcol_ref[8 * e + 2 * k + 1]], axis=1)
                for e in range(2)
            ],
            axis=0,
        )

    solve(rcol, 256, zh_ref, zl_ref, None)
    prod = mm3((yh_ref[...], yl_ref[...]), (zh_ref[...], zl_ref[...]), NT)
    for a in range(6):
        for e in range(2):
            part = prod[a * BS : (a + 1) * BS, e * BS : (e + 1) * BS]
            if a == 0:
                part = jnp.where(p < 8, 0.0, part)
            out_ref[a, e] = front_ref[a, e] - part

    for c in range(CHILD):
        k = at_ref[c]
        for s2 in range(8):
            h = bm_ref[k, (s2 % 4) * 16 + (s2 // 4) * 8 + q]
            b = h >> 3

            @pl.when(jnp.logical_and(h >= 0, (b >> 1) == step))
            def _(c=c, s2=s2, b=b, k=k):
                for t in range(4):
                    r = bm_ref[k, t * 16 + p]

                    @pl.when(r >= 0)
                    def _(r=r, s=c * 4 + t):
                        if s2 == 0:
                            blk = recv0_ref[s]
                        else:
                            blk = recv1_ref[s, :, (s2 - 1) * BS : s2 * BS]
                        out_ref[r >> 4, b & 1] += blk

    @pl.when(step == 0)
    def _():
        cs = pl.ds(pl.multiple_of(q * BS, BS), BS)
        for a in range(6):
            out_ref[a, 0] = yf_ref[a * BS : (a + 1) * BS, cs]

        @pl.when(p < 8)
        def _():
            out_ref[0, 0] = l_ref[pl.ds(pl.multiple_of(jnp.minimum(p, 7) * BS, BS), BS), cs]


def update(block_map, child_at, front, recv0, recv1, rrow, rcol, l, m):
    one = pl.Buffered(1)
    return pl.pallas_call(
        update_kernel,
        grid=(6,),
        out_shape=jax.ShapeDtypeStruct((6, 12, BS, BS), F32),
        in_specs=[
            SMEM_SPEC,
            SMEM_SPEC,
            pl.BlockSpec((6, 2, BS, BS), lambda i: (0, i, 0, 0)),
            pl.BlockSpec((16, BS, BS), lambda i: (0, 0, 0), pipeline_mode=one),
            pl.BlockSpec((16, BS, 7 * BS), lambda i: (0, 0, 0), pipeline_mode=one),
            pl.BlockSpec((8, 768, BS), lambda i: (0, 0, 0), pipeline_mode=one),
            pl.BlockSpec((16, BS, BS), lambda i: (0, i, 0)),
            pl.BlockSpec((1024, 1024), lambda i: (0, 0), pipeline_mode=one),
            pl.BlockSpec((4, 2 * BS, 2 * BS), lambda i: (0, 0, 0), pipeline_mode=one),
        ],
        out_specs=pl.BlockSpec((6, 2, BS, BS), lambda i: (0, i, 0, 0)),
        scratch_shapes=[
            pltpu.VMEM((1024, 1024), BF16),
            pltpu.VMEM((1024, 1024), BF16),
            pltpu.VMEM((4, 2 * BS, 2 * BS), BF16),
            pltpu.VMEM((4, 2 * BS, 2 * BS), BF16),
            pltpu.VMEM((768, 1024), F32),
            pltpu.VMEM((768, 1024), BF16),
            pltpu.VMEM((768, 1024), BF16),
            pltpu.VMEM((256, 1024), BF16),
            pltpu.VMEM((256, 1024), BF16),
        ],
        compiler_params=pltpu.CompilerParams(vmem_limit_bytes=60 * 1024 * 1024),
        cost_estimate=pl.CostEstimate(
            flops=18_000_000_000, bytes_accessed=36_000_000, transcendentals=0
        ),
        name="update",
    )(block_map, child_at, front, recv0, recv1, rrow, rcol, l, m)


def body(front, children, block_map, child_at):
    p = lax.axis_index("row")
    front4 = front.transpose(0, 2, 1, 3)
    slots = children.reshape(16, BS, 8 * BS)
    recv0 = lax.all_to_all(slots[:, :, :BS], "row", 0, 0)
    panel = assemble_panel(block_map, child_at, front4, recv0)
    low = lax.ppermute(panel[0, 64:], "row", [(i, i + 8) for i in range(8)])
    piece = jnp.where(p < 8, panel[0, :64], low)
    corner = lax.all_gather(piece, ("row", "col"))
    corner, panel, rest = lax.optimization_barrier((corner, panel, slots[:, :, BS:]))
    flat = panel.reshape(768, BS)
    moved = lax.ppermute(
        flat,
        ("row", "col"),
        [
            (r * 8 + c, ((r // 8) * 8 + c) * 8 + r % 8)
            for r in range(16)
            for c in range(8)
        ],
    )
    rcol = lax.all_gather(moved, "row")
    rrow = lax.all_gather(flat, "col")
    recv1 = lax.all_to_all(rest, "row", 0, 0)
    l, m = cholesky(corner)
    out = update(block_map, child_at, front4, recv0, recv1, rrow, rcol, l, m)
    return out.transpose(0, 2, 1, 3)


def solution(mesh):
    in_specs = (P(None, "row", None, "col"), P("row", "col"), P(), P())
    out_specs = P(None, "row", None, "col")
    return jax.shard_map(body, mesh=mesh, in_specs=in_specs, out_specs=out_specs, check_vma=False)
```

```python
import functools
import jax
import jax.numpy as jnp
from jax import lax
from jax.experimental import pallas as pl
from jax.experimental.pallas import tpu as pltpu
from jax.sharding import PartitionSpec as P

F32 = jnp.float32
BF16 = jnp.bfloat16
HIGHEST = lax.Precision.HIGHEST
CHILD = 4
BS = 128
NT = ((1,), (1,))
NN = ((1,), (0,))
VMEM_SPEC = pl.BlockSpec(memory_space=pltpu.VMEM)
SMEM_SPEC = pl.BlockSpec(memory_space=pltpu.SMEM)


def mm(a, b, dims):
    return lax.dot_general(a, b, (dims, ((), ())), precision=HIGHEST, preferred_element_type=F32)


def split(x):
    hi = x.astype(BF16)
    return hi, (x - hi.astype(F32)).astype(BF16)


def mm3(a, b, dims):
    dot = functools.partial(
        lax.dot_general, dimension_numbers=(dims, ((), ())), preferred_element_type=F32
    )
    return dot(a[0], b[0]) + (dot(a[0], b[1]) + dot(a[1], b[0]))


def diag_factor(get, put_u, put_x):
    sub = lax.broadcasted_iota(jnp.int32, (8, 128), 0)
    lane = lax.broadcasted_iota(jnp.int32, (8, 128), 1)
    d = [get(i) for i in range(16)]
    x = [(lane == sub + 8 * i).astype(F32) for i in range(16)]

    def panel(i, carry):
        d, x = list(carry[0]), list(carry[1])
        for j in range(8):
            c0 = jnp.broadcast_to(d[0][:, j:j + 1], (8, 128))
            r = lax.rsqrt(jnp.broadcast_to(c0[j:j + 1, :], (8, 128)))
            ud = jnp.broadcast_to(d[0][j:j + 1, :], (8, 128)) * r
            ux = jnp.broadcast_to(x[0][j:j + 1, :], (8, 128)) * r
            m = jnp.where(sub > j, c0 * r, 0.0)
            d[0] = jnp.where(sub == j, ud, d[0] - m * ud)
            x[0] = jnp.where(sub == j, ux, x[0] - m * ux)
            for k in range(1, 16):
                m = jnp.broadcast_to(d[k][:, j:j + 1], (8, 128)) * r
                d[k] = d[k] - m * ud
                x[k] = x[k] - m * ux
        row = d[0]
        row = pltpu.roll(row, 8 * i, 1)
        put_u(i, jnp.where(lane >= sub + 8 * i, row, 0.0))
        put_x(i, x[0])
        nd = [pltpu.roll(v, 120, 1) for v in d[1:]] + [jnp.zeros((8, 128), F32)]
        nx = x[1:] + [jnp.zeros((8, 128), F32)]
        return tuple(nd), tuple(nx)

    lax.fori_loop(0, 16, panel, (tuple(d), tuple(x)))


def chol_kernel(n, c_ref, l_ref, m_ref, u_ref, x_ref, hook):
    def blk(i, j):
        return (pl.ds(i * BS, BS), pl.ds(j * BS, BS))

    def corner(i, j):
        return jnp.concatenate([c_ref[i, j], c_ref[i + n, j]], axis=0)

    for i in range(n):
        for j in range(i + 1):
            l_ref[blk(i, j)] = 0.5 * (corner(i, j) + corner(j, i).T)
        for j in range(i + 1, n):
            l_ref[blk(i, j)] = jnp.zeros((BS, BS), F32)

    def put_u(i, v):
        u_ref[pl.ds(pl.multiple_of(8 * i, 8), 8), :] = v

    def put_x(i, v):
        x_ref[pl.ds(pl.multiple_of(8 * i, 8), 8), :] = v

    for k in range(n):
        diag_factor(lambda i, k=k: l_ref[pl.ds(k * BS + 8 * i, 8), pl.ds(k * BS, BS)], put_u, put_x)
        l_ref[blk(k, k)] = u_ref[...].T
        x = x_ref[...]
        h = k % 2
        m_ref[k // 2, h * BS : (h + 1) * BS, h * BS : (h + 1) * BS] = x
        if h == 1:
            m_ref[k // 2, 0:BS, BS : 2 * BS] = jnp.zeros((BS, BS), F32)
            t = mm(l_ref[blk(k, k - 1)], m_ref[k // 2, 0:BS, 0:BS], NN)
            m_ref[k // 2, BS : 2 * BS, 0:BS] = -mm(x, t, NN)
        if k == 2:
            hook()
        if k + 1 < n:
            lo = (k + 1) * BS
            rest = n * BS - lo
            col = mm(l_ref[pl.ds(lo, rest), pl.ds(k * BS, BS)], x, NT)
            l_ref[pl.ds(lo, rest), pl.ds(k * BS, BS)] = col
            for j in range(k + 1, n):
                o = (j - k - 1) * BS
                l_ref[pl.ds(j * BS, n * BS - j * BS), pl.ds(j * BS, BS)] -= mm(
                    col[o:], col[o : o + BS], NT
                )


ORDER = (
    (2, 2), (1, 1), (3, 3), (0, 2), (2, 0), (1, 3), (3, 1), (2, 1),
    (1, 2), (3, 2), (2, 3), (0, 1), (1, 0), (0, 3), (3, 0),
)
MESH = pl.DeviceIdType.MESH


def exchange_kernel(
    bm_ref, at_ref, front_ref, child_ref,
    recv0_ref, recv1_ref, rrow_ref, rcol_ref, l_ref, m_ref,
    small, panel, fr, c1, cbuf, seg, own, u_ref, x_ref, loc, snd, rcv,
):
    p = lax.axis_index("row")
    q = lax.axis_index("col")
    px, pz = p // 4, p % 4
    par = q % 2
    home = p % 8

    def peer(d):
        return ((px + d[0]) % 4) * 4 + (pz + d[1]) % 4

    def send(src, dst, i, to):
        pltpu.make_async_remote_copy(
            src_ref=src, dst_ref=dst, send_sem=snd.at[i], recv_sem=rcv.at[i],
            device_id=to, device_id_type=MESH,
        ).start()

    def local(src, dst, sem):
        return pltpu.make_async_copy(src, dst, sem)

    def wait(ref, sem):
        pltpu.make_async_copy(ref, ref, sem).wait()

    barrier = pltpu.get_barrier_semaphore()

    def hello(to):
        pl.semaphore_signal(barrier, inc=1, device_id=to, device_id_type=MESH)

    for d in ORDER:
        hello((peer(d), q))
    for i in range(1, 8):
        hello((p, (q + i) % 8))
    slot = (p // 8) * 8 + q

    @pl.when(home != q)
    def _():
        hello((slot, home))

    @pl.when(p >= 8)
    def _():
        for i in range(8):
            hello((p - 8, i))

    pl.semaphore_wait(barrier, 23 - jnp.where(home == q, 1, 0) + jnp.where(p < 8, 8, 0))

    for d in ORDER:
        send(child_ref.at[peer(d), :, pl.ds(0, BS)], small.at[p], 0, (peer(d), q))
    local(child_ref.at[p, :, pl.ds(0, BS)], small.at[p], rcv.at[0]).start()
    front_copy = local(front_ref.at[:, 0], fr, loc.at[0])
    front_copy.start()
    own_copy = local(child_ref.at[p, :, pl.ds(BS, 7 * BS)], own, loc.at[1])
    own_copy.start()
    front_copy.wait()
    wait(small, rcv.at[0])
    weights = []
    for c in range(CHILD):
        k = at_ref[c]
        hit = bm_ref[k, q] == q
        for t in range(4):
            r = bm_ref[k, t * 16 + p]
            weights.append(
                [jnp.where(jnp.logical_and(hit, r == a * 16 + p), 1.0, 0.0) for a in range(6)]
            )
    for a in range(6):
        acc = fr[a]
        for s in range(16):
            acc = acc + weights[s][a] * small[s]
        panel[a] = acc

    @pl.when(p < 8)
    def _():
        top, low = panel.at[0, pl.ds(0, 64)], panel.at[0, pl.ds(64, 64)]
        for i in range(1, 8):
            send(top, c1.at[q], 1, (p, (q + i) % 8))
        local(top, c1.at[q], rcv.at[1]).start()
        for i in range(8):
            send(low, c1.at[q], 1, (p + 8, (q + i) % 8))

    @pl.when(home == q)
    def _():
        local(panel, seg, rcv.at[4]).start()

    @pl.when(home != q)
    def _():
        send(panel, seg, 4, (slot, home))

    wait(c1, rcv.at[1])

    for b in range(2):
        half = pl.ds(par * 4 + 2 * b, 2)
        for d in ORDER:
            send(c1.at[half], cbuf.at[p, half], 3, (peer(d), q))
        local(c1.at[half], cbuf.at[p, half], rcv.at[3]).start()

    def send_rows(a, carry):
        rows = pl.ds(pl.multiple_of(a * BS, BS), BS)
        for i in range(1, 8):
            send(panel.at[a], rrow_ref.at[q, rows], 2, (p, (q + i) % 8))
        local(panel.at[a], rrow_ref.at[q, rows], rcv.at[2]).start()
        return carry

    mine = cbuf.at[:, pl.ds(par * 4, 4)]
    wait(mine, rcv.at[3])
    send(mine, mine, 5, (p, q + 1 - 2 * par))
    lax.fori_loop(0, 6, send_rows, 0)

    upper, lower = pl.ds(0, 3), pl.ds(3, 3)
    wait(seg, rcv.at[4])
    for i in range(1, 4):
        send(seg.at[upper], rcol_ref.at[px, pz, upper], 7, (peer((0, i)), q))
        send(seg.at[lower], rcol_ref.at[px, pz, lower], 7, (peer((i, 0)), q))
    seg_copy = local(seg, rcol_ref.at[px, pz], loc.at[0])
    seg_copy.start()

    def forward():
        wait(rcol_ref.at[0, pl.ds(0, 3)], rcv.at[7])
        seg_copy.wait()
        for j in range(4):
            for i in range(1, 4):
                piece = rcol_ref.at[px, j, upper]
                send(piece, piece, 8, (peer((i, 0)), q))
                piece = rcol_ref.at[j, pz, lower]
                send(piece, piece, 8, (peer((0, i)), q))

    def send_slots(c, carry):
        rows = pl.ds(pl.multiple_of(c * 16, 16), 16)
        cols = pl.ds(BS, 7 * BS)
        for d in ORDER:
            send(child_ref.at[peer(d), rows, cols], recv1_ref.at[p, rows], 6, (peer(d), q))
        return carry

    lax.fori_loop(0, 8, send_slots, 0)
    own_copy.wait()
    local(own, recv1_ref.at[p], rcv.at[6]).start()
    recv0_copy = local(small, recv0_ref, loc.at[1])
    recv0_copy.start()
    wait(cbuf.at[:, pl.ds(4 - par * 4, 4)], rcv.at[5])
    chol_kernel(8, cbuf, l_ref, m_ref, u_ref, x_ref, forward)
    recv0_copy.wait()
    wait(rrow_ref, rcv.at[2])
    wait(rcol_ref.at[pl.ds(0, 3)], rcv.at[8])
    wait(recv1_ref, rcv.at[6])
    wait(small.at[pl.ds(0, 15)], snd.at[0])
    wait(rrow_ref.at[pl.ds(0, 7)], snd.at[2])
    wait(cbuf.at[pl.ds(0, 15), pl.ds(0, 4)], snd.at[3])
    wait(rcol_ref.at[0, pl.ds(0, 3)], snd.at[7])
    wait(rcol_ref.at[pl.ds(0, 3)], snd.at[8])

    @pl.when(p < 8)
    def _():
        wait(c1, snd.at[1])
        wait(c1.at[pl.ds(0, 7)], snd.at[1])

    @pl.when(home != q)
    def _():
        wait(seg, snd.at[4])

    wait(mine, snd.at[5])
    wait(recv1_ref.at[pl.ds(0, 15)], snd.at[6])


def exchange(block_map, child_at, front, children):
    any_spec = pl.BlockSpec(memory_space=pl.ANY)
    return pl.pallas_call(
        exchange_kernel,
        out_shape=(
            jax.ShapeDtypeStruct((16, BS, BS), F32),
            jax.ShapeDtypeStruct((16, BS, 7 * BS), F32),
            jax.ShapeDtypeStruct((8, 6 * BS, BS), F32),
            jax.ShapeDtypeStruct((4, 4, 6, BS, BS), F32),
            jax.ShapeDtypeStruct((8 * BS, 8 * BS), F32),
            jax.ShapeDtypeStruct((4, 2 * BS, 2 * BS), F32),
        ),
        in_specs=[SMEM_SPEC, SMEM_SPEC, any_spec, any_spec],
        out_specs=(any_spec, any_spec, any_spec, any_spec, VMEM_SPEC, VMEM_SPEC),
        scratch_shapes=[
            pltpu.VMEM((16, BS, BS), F32),
            pltpu.VMEM((6, BS, BS), F32),
            pltpu.VMEM((6, BS, BS), F32),
            pltpu.VMEM((8, 64, BS), F32),
            pltpu.VMEM((16, 8, 64, BS), F32),
            pltpu.VMEM((6, BS, BS), F32),
            pltpu.VMEM((BS, 7 * BS), F32),
            pltpu.VMEM((BS, BS), F32),
            pltpu.VMEM((BS, BS), F32),
            pltpu.SemaphoreType.DMA((2,)),
            pltpu.SemaphoreType.DMA((9,)),
            pltpu.SemaphoreType.DMA((9,)),
        ],
        compiler_params=pltpu.CompilerParams(
            collective_id=1, has_side_effects=True, vmem_limit_bytes=60 * 1024 * 1024
        ),
        name="exchange",
    )(block_map, child_at, front, children)


def update_kernel(
    bm_ref, at_ref, front_ref, recv0_ref, recv1_ref, rrow_ref, rcol_ref, l_ref, m_ref, out_ref,
    lh_ref, ll_ref, mh_ref, ml_ref, yf_ref, yh_ref, yl_ref, zh_ref, zl_ref,
):
    step = pl.program_id(0)
    p = lax.axis_index("row")
    q = lax.axis_index("col")
    W = 2 * BS

    def solve(rhs, rows, yh, yl, yf):
        for k in range(4):
            t = rhs(k)
            for j in range(k):
                js = pl.ds(j * W, W)
                ks = pl.ds(k * W, W)
                t = t - mm3((yh[:, js], yl[:, js]), (lh_ref[ks, js], ll_ref[ks, js]), NT)
            y = mm3(split(t), (mh_ref[k], ml_ref[k]), NT)
            ks = pl.ds(k * W, W)
            if yf is not None:
                yf[:, ks] = y
            yh[:, ks], yl[:, ks] = split(y)

    @pl.when(step == 0)
    def _():
        for k in range(4):
            mh_ref[k], ml_ref[k] = split(m_ref[k])
            for j in range(k):
                js = pl.ds(j * W, W)
                ks = pl.ds(k * W, W)
                lh_ref[ks, js], ll_ref[ks, js] = split(l_ref[ks, js])
        solve(
            lambda k: jnp.concatenate([rrow_ref[2 * k], rrow_ref[2 * k + 1]], axis=1),
            768, yh_ref, yl_ref, yf_ref,
        )

    def rcol(k):
        return jnp.concatenate(
            [
                jnp.concatenate([rcol_ref[8 * e + 2 * k], rcol_ref[8 * e + 2 * k + 1]], axis=1)
                for e in range(2)
            ],
            axis=0,
        )

    solve(rcol, 256, zh_ref, zl_ref, None)
    prod = mm3((yh_ref[...], yl_ref[...]), (zh_ref[...], zl_ref[...]), NT)
    for a in range(6):
        for e in range(2):
            part = prod[a * BS : (a + 1) * BS, e * BS : (e + 1) * BS]
            if a == 0:
                part = jnp.where(p < 8, 0.0, part)
            out_ref[a, e] = front_ref[a, e] - part

    for c in range(CHILD):
        k = at_ref[c]
        for s2 in range(8):
            h = bm_ref[k, (s2 % 4) * 16 + (s2 // 4) * 8 + q]
            b = h >> 3

            @pl.when(jnp.logical_and(h >= 0, (b >> 1) == step))
            def _(c=c, s2=s2, b=b, k=k):
                for t in range(4):
                    r = bm_ref[k, t * 16 + p]

                    @pl.when(r >= 0)
                    def _(r=r, s=c * 4 + t):
                        if s2 == 0:
                            blk = recv0_ref[s]
                        else:
                            blk = recv1_ref[s, :, (s2 - 1) * BS : s2 * BS]
                        out_ref[r >> 4, b & 1] += blk

    @pl.when(step == 0)
    def _():
        cs = pl.ds(pl.multiple_of(q * BS, BS), BS)
        for a in range(6):
            out_ref[a, 0] = yf_ref[a * BS : (a + 1) * BS, cs]

        @pl.when(p < 8)
        def _():
            out_ref[0, 0] = l_ref[pl.ds(pl.multiple_of(jnp.minimum(p, 7) * BS, BS), BS), cs]


def update(block_map, child_at, front, recv0, recv1, rrow, rcol, l, m):
    one = pl.Buffered(1)
    return pl.pallas_call(
        update_kernel,
        grid=(6,),
        out_shape=jax.ShapeDtypeStruct((6, 12, BS, BS), F32),
        in_specs=[
            SMEM_SPEC,
            SMEM_SPEC,
            pl.BlockSpec((6, 2, BS, BS), lambda i: (0, i, 0, 0)),
            pl.BlockSpec((16, BS, BS), lambda i: (0, 0, 0), pipeline_mode=one),
            pl.BlockSpec((16, BS, 7 * BS), lambda i: (0, 0, 0), pipeline_mode=one),
            pl.BlockSpec((8, 768, BS), lambda i: (0, 0, 0), pipeline_mode=one),
            pl.BlockSpec((16, BS, BS), lambda i: (0, i, 0)),
            pl.BlockSpec((1024, 1024), lambda i: (0, 0), pipeline_mode=one),
            pl.BlockSpec((4, 2 * BS, 2 * BS), lambda i: (0, 0, 0), pipeline_mode=one),
        ],
        out_specs=pl.BlockSpec((6, 2, BS, BS), lambda i: (0, i, 0, 0)),
        scratch_shapes=[
            pltpu.VMEM((1024, 1024), BF16),
            pltpu.VMEM((1024, 1024), BF16),
            pltpu.VMEM((4, 2 * BS, 2 * BS), BF16),
            pltpu.VMEM((4, 2 * BS, 2 * BS), BF16),
            pltpu.VMEM((768, 1024), F32),
            pltpu.VMEM((768, 1024), BF16),
            pltpu.VMEM((768, 1024), BF16),
            pltpu.VMEM((256, 1024), BF16),
            pltpu.VMEM((256, 1024), BF16),
        ],
        compiler_params=pltpu.CompilerParams(vmem_limit_bytes=60 * 1024 * 1024),
        cost_estimate=pl.CostEstimate(
            flops=18_000_000_000, bytes_accessed=36_000_000, transcendentals=0
        ),
        name="update",
    )(block_map, child_at, front, recv0, recv1, rrow, rcol, l, m)


def body(front, children, block_map, child_at):
    front4 = front.transpose(0, 2, 1, 3)
    recv0, recv1, rrow, rcol, l, m = exchange(
        block_map, child_at, front4, children.reshape(16, BS, 8 * BS)
    )
    out = update(block_map, child_at, front4, recv0, recv1, rrow, rcol.reshape(16, 6 * BS, BS), l, m)
    return out.transpose(0, 2, 1, 3)


def solution(mesh):
    in_specs = (P(None, "row", None, "col"), P("row", "col"), P(), P())
    out_specs = P(None, "row", None, "col")
    return jax.shard_map(body, mesh=mesh, in_specs=in_specs, out_specs=out_specs, check_vma=False)
```
